128 devices in a mesh: gx: 16 (over z, y), gy: 8 (over x, core).
Axes of the slice: x: 4, y: 4, z: 4, core: 2. Of those that a mesh axis runs over, the one named last changes fastest.
Arguments:
- density: float32 [512, 256, 512], P('gx', 'gy'), may hold values from 0.5 to 2
- momentum: float32 [3, 512, 256, 512], P(None, 'gx', 'gy'), may hold values from -3 to 3
- energy: float32 [512, 256, 512], P('gx', 'gy'), may hold values from 2 to 4
- coarse_rows: float32 [2, 4096, 8, 160], P(None, 'gx', 'gy'), may hold values from -2 to 4, as said below
- ghost_rows: int32 [8, 16, 128], P('gy'), may hold values from 0 to 4095, as said below
- time_index: int32 [8, 16, 128], P('gy'), may hold values from 0 to 8
Outputs:
- section_state: float32 [5, 512, 256, 512], P(None, 'gx', 'gy')
The draws below stay inside these ranges and needn't reach their ends.
Inputs may be any that keep to these rules, and one draw needn't show every extreme that they name: `ghost_rows`: entry [b, a, s] names a coarse row of column b; rows c * 256 to (c + 1) * 256 - 1 of a column lie on the device with gx index c. Exactly 8 of one device's slots name rows held by each source device. `coarse_rows`: field 0 of every row (density) lies in 0.5 to 2.
All inputs are finite; a program needn't handle non-finite values.
Results may differ from the reference program's by a relative error of at most 0.0003.
Values sent between devices are 32-bit elements; how exact they have to be, the bound alone decides.
No kernel may reach another device: no remote copies, remote signals or barrier semaphores. Data moves between devices by JAX's collectives and lax.ppermute only.
A program may use at most 256 MiB of HBM per device.

```python
import jax
import jax.numpy as jnp
from jax import lax

CXY = 32
CZ = 512
CROW = 256
NX = 512
NY = 256
COARSE_ROWS = 4096
GHOST_SLOTS = 128
N_GX = 16
N_GY = 8


def draw_coarse_rows(key, part):
    key_rho = jax.random.fold_in(key, 11)
    key_mom = jax.random.fold_in(key, 12)
    key_ene = jax.random.fold_in(key, 13)
    rho_part = jax.random.uniform(key_rho, (2, COARSE_ROWS, N_GY, 1, CXY), jnp.float32, 0.5, 2.0)
    mom_part = jnp.clip(0.5 * jax.random.normal(key_mom, (2, COARSE_ROWS, N_GY, 3, CXY), jnp.float32), -2.0, 2.0)
    ene_part = jax.random.uniform(key_ene, (2, COARSE_ROWS, N_GY, 1, CXY), jnp.float32, 2.0, 4.0)
    joined = jnp.concatenate([rho_part, mom_part, ene_part], axis=3)
    return joined.reshape(2, COARSE_ROWS, N_GY, 5 * CXY).astype(jnp.float32)


def draw_ghost_rows(key, part):
    capacity = 4 * CXY // N_GX
    base_device = jax.random.randint(jax.random.fold_in(key, 21), (N_GY, N_GX, 1), 0, N_GX)
    row_offset = jax.random.randint(jax.random.fold_in(key, 22), (N_GY, N_GX, 4 * CXY), 0, CROW)
    slot_ids = jnp.arange(4 * CXY, dtype=jnp.int32)
    side_of = slot_ids // (2 * CXY)
    within = slot_ids % (2 * CXY)
    offset_src = jnp.where(side_of >= 1, N_GX // 2, 0)
    source = (base_device + offset_src + within // capacity) % N_GX
    return (source * CROW + row_offset).astype(jnp.int32)


def place_ends(values, stream_key, low, largest):
    longest = values.shape.index(max(values.shape))
    spots = []
    for shift in (0, 1):
        where = [jax.random.randint(jax.random.fold_in(stream_key, axis), (), 0, length) for axis, length in enumerate(values.shape)]
        where[longest] = (where[longest] + shift) % values.shape[longest]
        spots.append(tuple(where))
    return values.at[spots[0]].set(low).at[spots[1]].set(largest)


def levels(key, dims, pieces, least, high):
    level = 1.0
    for dim, blocks in pieces:
        heights = jax.random.uniform(jax.random.fold_in(jax.random.fold_in(key, 6), dim), (blocks,), jnp.float32, least / len(pieces), high / len(pieces))
        level = level * jnp.repeat(jnp.exp(heights), dims[dim] // blocks).reshape((-1,) + (1,) * (len(dims) - 1 - dim))
    return level


def normal_values(stream_key, dims, spread, reach, pieces=(), held_as=jnp.bfloat16):
    drawn = jax.random.normal(stream_key, dims, jnp.float32) * spread
    if len(pieces) > 0:
        drawn = levels(stream_key, dims, pieces, -0.22, 0.18) * drawn
    return jnp.clip(drawn, min=-reach, max=reach).astype(held_as)


def setup_inputs(seed: int = 0) -> dict:
    splits = jax.random.split(jax.random.key(seed), 7)
    density = jnp.clip(0.5 + 1.5 * jax.random.uniform(splits[0], (NX, NY, CZ), jnp.float32) ** levels(splits[0], (NX, NY, CZ), ((0, 16), (1, 8)), -0.2, 0.2), 0.5, 2.0)
    momentum = normal_values(splits[1], (3, NX, NY, CZ), 0.5, 3.0, ((1, 16), (2, 8)), jnp.float32)
    energy = jnp.clip(2.0 + 2.0 * jax.random.uniform(splits[2], (NX, NY, CZ), jnp.float32) ** levels(splits[2], (NX, NY, CZ), ((0, 16), (1, 8)), -0.2, 0.2), 2.0, 4.0)
    coarse_rows = draw_coarse_rows(jax.random.fold_in(splits[6], 71), 0)
    ghost_rows = draw_ghost_rows(jax.random.fold_in(splits[6], 71), 0)
    time_index = place_ends(jax.random.randint(splits[5], (N_GY, N_GX, GHOST_SLOTS), 0, 9), jax.random.fold_in(splits[5], 1), 0, 8).astype(jnp.int32)
    return dict(density=density, momentum=momentum, energy=energy, coarse_rows=coarse_rows, ghost_rows=ghost_rows, time_index=time_index)


beta_coef = 1.0 / 3.0
a_coef = 14.0 / 9.0
b_coef = 1.0 / 9.0
gamma_gas = 1.4
time_step = 0.4

def fluxes(fields, direction):
    density = fields[0]
    carried = fields[1 + direction]
    velocity = carried / density
    kinetic = (fields[1] * fields[1] + fields[2] * fields[2] + fields[3] * fields[3]) / density
    pressure = (gamma_gas - 1.0) * (fields[4] - 0.5 * kinetic)
    columns = [carried]
    for component in range(3):
        product_term = fields[1 + component] * velocity
        if component == direction:
            product_term = product_term + pressure
        columns.append(product_term)
    columns.append((fields[4] + pressure) * velocity)
    return jnp.stack(columns)

def stencil(extended, line_axis, length):

    def window(offset):
        return lax.slice_in_dim(extended, offset, offset + length, axis=line_axis)
    return 0.5 * a_coef * (window(3) - window(1)) + 0.25 * b_coef * (window(4) - window(0))

def interpolate(coarse_column, row_ids, level_index):
    safe_rows = jnp.maximum(row_ids, 0)
    picked_old = coarse_column[0][safe_rows]
    picked_new = coarse_column[1][safe_rows]
    weight = (level_index.astype(jnp.float32) * 0.125)[..., None]
    blended = (1.0 - weight) * picked_old + weight * picked_new
    return jnp.where((row_ids >= 0)[..., None], blended, 0.0)

def ghost_layers(coarse_rows, ghost_rows, time_index):
    values = jax.vmap(interpolate, in_axes=(2, 0, 0))(coarse_rows, ghost_rows, time_index)
    values = values.reshape(N_GY, N_GX, 4, CXY, 5, CXY).transpose(4, 1, 3, 0, 5, 2)
    return values.reshape(5, NX, NY, 4)

def solve_lines(right, line_axis):
    length = right.shape[line_axis]
    positions = jnp.arange(length)
    distance = jnp.abs(positions[:, None] - positions[None, :])
    matrix = jnp.where(distance == 0, 1.0, jnp.where(distance == 1, beta_coef, 0.0)).astype(jnp.float32)
    moved = jnp.moveaxis(right, line_axis, 0)
    flattened = moved.reshape(length, -1)
    solved = jnp.linalg.solve(matrix, flattened)
    return jnp.moveaxis(solved.reshape(moved.shape), 0, line_axis)

def reference(density, momentum, energy, coarse_rows, ghost_rows, time_index):
    fields = jnp.concatenate([density[None], momentum, energy[None]], axis=0)
    layers = ghost_layers(coarse_rows, ghost_rows, time_index)
    extended_z = jnp.concatenate([layers[..., 0:2], fields, layers[..., 2:4]], axis=3)
    flux_x = jnp.pad(fluxes(fields, 0), ((0, 0), (2, 2), (0, 0), (0, 0)))
    flux_y = jnp.pad(fluxes(fields, 1), ((0, 0), (0, 0), (2, 2), (0, 0)))
    flux_z = fluxes(extended_z, 2)
    deriv_x = solve_lines(stencil(flux_x, 1, NX), 1)
    deriv_y = solve_lines(stencil(flux_y, 2, NY), 2)
    deriv_z = solve_lines(stencil(flux_z, 3, CZ), 3)
    return fields - time_step * (deriv_x + deriv_y + deriv_z)
```

```python
import functools
import math

import jax
import jax.numpy as jnp
import ml_dtypes
import numpy as np
from jax import lax
from jax.experimental import pallas as pl
from jax.experimental.pallas import tpu as pltpu
from jax.sharding import PartitionSpec as P

BETA = 1.0 / 3.0
NEAR = 7.0 / 9.0
FAR = 1.0 / 36.0
STEP = 0.4
KAPPA = math.sqrt(1.0 - 4.0 * BETA * BETA)
ROOT = (-1.0 + KAPPA) / (2.0 * BETA)
TAIL = (NEAR * (1.0 / ROOT - ROOT) + FAR * (1.0 / ROOT**2 - ROOT**2)) / KAPPA
FIRST = (NEAR * (1.0 - ROOT**2) + FAR * (ROOT - ROOT**3)) / KAPPA
SCALE = 1.253065
B = 32
NZ = 512
F32 = jnp.float32
BF16 = jnp.bfloat16
highest = lax.Precision.HIGHEST


@functools.cache
def derivative_matrix(length):
    extended = np.zeros((length, length + 4))
    rows = np.arange(length)
    extended[rows, rows + 3] += NEAR
    extended[rows, rows + 1] -= NEAR
    extended[rows, rows + 4] += FAR
    extended[rows, rows] -= FAR
    left = np.eye(length) + BETA * (np.eye(length, k=1) + np.eye(length, k=-1))
    return np.linalg.solve(left, extended)


def rounded(matrix):
    return np.asarray(matrix, np.float32).astype(ml_dtypes.bfloat16)


def block_matrix(outer):
    place = np.arange(B)
    gap = place[None, :] - place[:, None]
    size = np.abs(gap).astype(float)
    entry = np.where(size == 0, 0.0, np.where(size == 1, FIRST, TAIL * ROOT**size))

    def spread(part):
        part = np.kron(np.eye(8), part) if outer else np.kron(part, np.eye(8))
        part = part.reshape(-1, 32, 1, 8)
        return np.concatenate([part, part], axis=2).reshape(-1, 512)

    right, left = ROOT ** (B - 1.0 - place), ROOT ** (place * 1.0)
    rows = [spread(np.sign(gap) * entry * SCALE)]
    rows += [spread(w[None]).astype(np.float32) for w in (right, left)]
    rows += [spread((w - rounded(w).astype(float))[None]) for w in (right, left)]
    rows += [spread((place == at)[None] * 1.0) for at in (B - 1, 0)]
    return rounded(np.concatenate(rows, axis=0))


def z_matrix():
    return rounded(derivative_matrix(NZ)[:, 2:-2].T * SCALE)


def ghost_matrix():
    full = derivative_matrix(NZ)
    table = np.zeros((4, 256))
    table[0:2, :128] = full[:128, 0:2].T
    table[2:4, 128:] = full[-128:, -2:].T
    table = np.asarray(-STEP * np.repeat(table, 8, axis=0), np.float32)
    high = rounded(table)
    low = rounded(table - high.astype(np.float32))
    return np.concatenate([high, high, low], axis=0)


def edge_weights():
    place = np.arange(B)
    table = np.zeros((4, B))
    table[0] = STEP * TAIL * ROOT ** (place + 1.0)
    table[1, 0] = STEP * (FIRST - TAIL * ROOT)
    table[2] = -STEP * TAIL * ROOT ** (B - place * 1.0)
    table[3, -1] = -STEP * (FIRST - TAIL * ROOT)
    return table.astype(np.float32)


def state_parts(density, m1, m2, m3, energy):
    inverse = 1.0 / density
    u1, u2, u3 = m1 * inverse, m2 * inverse, m3 * inverse
    pressure = 0.4 * energy - 0.2 * (m1 * u1 + m2 * u2 + m3 * u3)
    return u1, u2, u3, pressure


def split(value):
    high = value.astype(BF16)
    return high, (value - high.astype(F32)).astype(BF16)


def halves(value):
    high = value.astype(BF16).astype(F32)
    both = jnp.concatenate([high, value - high], axis=1).astype(BF16)
    return both.reshape(-1, 128)


PIECES = 7
ANYWHERE = pl.BlockSpec(memory_space=pl.ANY)
IN_VMEM = pl.BlockSpec(memory_space=pltpu.VMEM)


def piece_slices(k):
    xs = 2 * (k // 8)
    yh = (k // 4) % 2
    ys = pl.ds(pl.multiple_of(16 * yh, 16), 16)
    zs = pl.ds(pl.multiple_of(128 * (k % 4), 128), 128)
    return xs, yh, ys, zs


def state_copies(rho, mom, ene, state, sems, i, first=0):
    xs = pl.ds(8 * (first + i), 8)
    to = pl.ds(8 * i, 8)
    return (
        pltpu.make_async_copy(rho.at[xs], state.at[0, to], sems.at[i, 0]),
        pltpu.make_async_copy(mom.at[:, xs], state.at[1:4, to], sems.at[i, 1]),
        pltpu.make_async_copy(ene.at[xs], state.at[4, to], sems.at[i, 2]),
    )


def xy_kernel(rho, mom, ene, kx, ky, after, part, xr, xl, yr, yl, fbuf, g0, g1, sems):
    factor = STEP / SCALE
    copies = [state_copies(rho, mom, ene, part, sems, i) for i in range(4)]
    for group in copies:
        for copy in group:
            copy.start()

    def piece(i, k, gbuf):
        xp, yh, ys, zs = piece_slices(k)
        xs = pl.ds(8 * i + xp, 2)
        d, m1, m2, m3, e = (part[c, xs, ys, zs].reshape(4, 8, 128) for c in range(5))
        u1, u2, u3, p = state_parts(d, m1, m2, m3, e)
        ep = e + p
        cross = halves(m1 * u2)
        f = (halves(m1), halves(m1 * u1 + p), cross, halves(m3 * u1), halves(ep * u1))
        g = (halves(m2), cross, halves(m2 * u2 + p), halves(m3 * u2), halves(ep * u2))
        for c in range(5):
            for x2 in range(2):
                frow = pl.multiple_of(128 * i + 16 * xp + 16 * x2, 16)
                for y8 in range(2):
                    at = 32 * x2 + 16 * y8
                    fbuf[c, 2 * yh + y8, pl.ds(frow, 16), zs] = f[c][at : at + 16]
                row = pl.multiple_of(64 * xp + 64 * x2 + 32 * yh, 32)
                gbuf[c, pl.ds(row, 32), zs] = g[c][32 * x2 : 32 * x2 + 32]

    def keep(right, left, c, rows, result):
        extra = result[256:]
        right[c, rows] = extra[0:8] + extra[16:24]
        left[c, rows] = extra[8:16] + extra[24:32]
        right[5 + c, rows] = extra[32:40]
        left[5 + c, rows] = extra[40:48]

    gs = (g0, g1)
    for i in range(5):
        if i < 4:
            for copy in copies[i]:
                copy.wait()

        def stage(c, carry, i=i):
            if i < 4:
                for j in range(PIECES):
                    piece(i, jnp.minimum(PIECES * c + j, 31), gs[i % 2])
            if i >= 1:
                xs = pl.ds(8 * (i - 1), 8)
                across = jnp.dot(ky[...], gs[(i - 1) % 2][c], preferred_element_type=F32)
                part[c, xs] = part[c, xs] - factor * across[:256].reshape(8, B, NZ)
                keep(yr, yl, c, xs, across)
            return carry

        lax.fori_loop(0, 5, stage, 0)

    def last(c, carry):
        for block in range(4):
            ys = pl.ds(8 * block, 8)
            slope = jnp.dot(kx[...], fbuf[c, block], preferred_element_type=F32)
            part[c, :, ys, :] = part[c, :, ys, :] - factor * slope[:256].reshape(B, 8, NZ)
            keep(xr, xl, c, ys, slope)
        return carry

    lax.fori_loop(0, 5, last, 0)


def xy_part(rho, mom, ene, after):
    return pl.pallas_call(
        xy_kernel,
        in_specs=[ANYWHERE] * 3 + [IN_VMEM] * 2 + [ANYWHERE],
        out_specs=[IN_VMEM] * 5,
        out_shape=[pltpu.VMEM((5, B, B, NZ), F32)] + [pltpu.VMEM((10, B, NZ), F32)] * 4,
        scratch_shapes=[
            pltpu.VMEM((5, 4, 512, NZ), BF16),
            pltpu.VMEM((5, 512, NZ), BF16),
            pltpu.VMEM((5, 512, NZ), BF16),
            pltpu.SemaphoreType.DMA((4, 3)),
        ],
        compiler_params=pltpu.CompilerParams(vmem_limit_bytes=24 << 20),
        name="xy_part",
    )(rho, mom, ene, jnp.asarray(block_matrix(False)), jnp.asarray(block_matrix(True)), after)


def z_kernel(first, start, rho, mom, ene, mz, after, part, state, h0, h1, sems):
    factor = STEP / SCALE
    copies = [state_copies(rho, mom, ene, state, sems, i, first) for i in range(2)]
    for group in copies:
        for copy in group:
            copy.start()

    def piece(i, k, hbuf):
        xp, yh, ys, zs = piece_slices(k)
        xs = pl.ds(8 * i + xp, 2)
        d, m1, m2, m3, e = (state[c, xs, ys, zs].reshape(4, 8, 128) for c in range(5))
        u1, u2, u3, p = state_parts(d, m1, m2, m3, e)
        h = [halves(v) for v in (m3, m1 * u3, m2 * u3, m3 * u3 + p, (e + p) * u3)]
        for c in range(5):
            for x2 in range(2):
                row = pl.multiple_of(64 * xp + 64 * x2 + 32 * yh, 32)
                hbuf[c, pl.ds(row, 32), zs] = h[c][32 * x2 : 32 * x2 + 32]

    hs = (h0, h1)
    for i in range(3):
        if i < 2:
            for copy in copies[i]:
                copy.wait()

        def stage(c, carry, i=i):
            if i < 2:
                for j in range(PIECES):
                    piece(i, jnp.minimum(PIECES * c + j, 31), hs[i % 2])
            if i >= 1:
                xs = pl.ds(8 * (first + i - 1), 8)
                along = jnp.dot(hs[(i - 1) % 2][c], mz[...], preferred_element_type=F32)
                along = along.reshape(32, 2, 8, NZ)
                along = along[:, 0] + along[:, 1]
                part[c, xs] = part[c, xs] - factor * along.reshape(8, B, NZ)
            return carry

        lax.fori_loop(0, 5, stage, 0)


def z_part(first, part, rho, mom, ene, after):
    return pl.pallas_call(
        functools.partial(z_kernel, first),
        in_specs=[IN_VMEM] + [ANYWHERE] * 3 + [IN_VMEM, ANYWHERE],
        out_specs=IN_VMEM,
        out_shape=pltpu.VMEM((5, B, B, NZ), F32),
        input_output_aliases={0: 0},
        scratch_shapes=[
            pltpu.VMEM((5, 16, B, NZ), F32),
            pltpu.VMEM((5, 512, NZ), BF16),
            pltpu.VMEM((5, 512, NZ), BF16),
            pltpu.SemaphoreType.DMA((2, 3)),
        ],
        compiler_params=pltpu.CompilerParams(vmem_limit_bytes=20 << 20),
        name="z_part",
    )(part, rho, mom, ene, jnp.asarray(z_matrix()), after)


def merge_kernel(kept, got, after, stay, leave):
    for h, source in enumerate((kept, got)):
        for a in range(4):
            to = pl.ds(32 * h + 8 * a, 8)
            stay[to, :] = source[pl.ds(16 * a, 8), :]
            leave[to, :] = source[pl.ds(16 * a + 8, 8), :]


def merge(kept, got, after):
    return pl.pallas_call(
        merge_kernel,
        in_specs=[IN_VMEM] * 2 + [ANYWHERE],
        out_specs=[IN_VMEM] * 2,
        out_shape=[pltpu.VMEM((64, 160), F32)] * 2,
        compiler_params=pltpu.CompilerParams(vmem_limit_bytes=1 << 20),
        name="merge_rows",
    )(kept, got, after)


def ghost_kernel(pick, kept, got, out):
    ghosts = jnp.dot(pick[:, 0:64], kept[...], precision=highest, preferred_element_type=F32)
    ghosts = ghosts + jnp.dot(pick[:, 64:128], got[...], precision=highest, preferred_element_type=F32)
    d, m1, m2, m3, e = (ghosts[:, 32 * c : 32 * c + 32] for c in range(5))
    u1, u2, u3, p = state_parts(d, m1, m2, m3, e)
    cell = lax.broadcasted_iota(jnp.int32, (128, 256), 0) % 8
    lane = lax.broadcasted_iota(jnp.int32, (128, 256), 1) // 32
    for c, h in enumerate((m3, m1 * u3, m2 * u3, m3 * u3 + p, (e + p) * u3)):
        out[c] = jnp.where(cell == lane, jnp.concatenate([h] * 8, axis=1), 0.0)


def ghost_flux(pick, kept, got):
    return pl.pallas_call(
        ghost_kernel,
        in_specs=[IN_VMEM] * 3,
        out_specs=IN_VMEM,
        out_shape=pltpu.VMEM((5, 128, 256), F32),
        compiler_params=pltpu.CompilerParams(vmem_limit_bytes=4 << 20),
        name="ghost_flux",
    )(pick, kept, got)


GROUP = 8


def finish_kernel(table, part, fl, fr, gl, gr, xr, xl, yr, yl, wy, ghost, mg, out, el, er, hl, hr, wu, slots, sems):
    inner = []
    place = lax.axis_index("gx"), lax.axis_index("gy")
    for at_end, own, got, kept in (
        (place[0] == 0, xl, fl, el),
        (place[0] == 15, xr, fr, er),
        (place[1] == 0, yl, gl, hl),
        (place[1] == 7, yr, gr, hr),
    ):
        inner.append(jnp.where(at_end, 0.0, 1.0).astype(F32))

        @pl.when(at_end)
        def _(own=own, kept=kept):
            for c in range(5):
                kept[c] = ROOT * own[c] + ((FIRST - TAIL * ROOT) / TAIL) * own[5 + c]

        @pl.when(jnp.logical_not(at_end))
        def _(got=got, kept=kept):
            for c in range(5):
                kept[c] = got[c]

    wu[0] = wy[0]
    wu[1] = wy[1] * inner[2]
    wu[2] = wy[2]
    wu[3] = wy[3] * inner[3]

    def group(step, carry):
        slot = step % 2
        xs = pl.ds(GROUP * step, GROUP)

        def copy_out(at):
            return pltpu.make_async_copy(slots.at[slot], out.at[:, pl.ds(GROUP * at, GROUP)], sems.at[slot])

        @pl.when(step >= 2)
        def _():
            copy_out(step - 2).wait()

        aligned = pl.ds(pl.multiple_of(GROUP * step, GROUP), GROUP)
        for c in range(5):
            lines = [ghost[c, pl.ds(pl.multiple_of(32 * k + GROUP * step, 8), 8), :] for k in range(4)]
            high, low = split(jnp.concatenate(lines, axis=0))
            zpart = lax.dot_general(
                jnp.concatenate([high, low, high], axis=0),
                mg[...],
                (((0,), (0,)), ((), ())),
                preferred_element_type=F32,
            )
            for q in range(4):
                zs = pl.ds(128 * q, 128)
                low, high = hl[c, aligned, zs], hr[c, aligned, zs]
                low_edge, high_edge = gl[5 + c, aligned, zs], gr[5 + c, aligned, zs]
                for k in range(GROUP):
                    x = GROUP * step + k
                    ql = table[0, x]
                    qr = table[2, x]
                    for t in range(4):
                        rows = pl.ds(8 * t, 8)
                        value = part[c, x, rows, zs] + ql * el[c, rows, zs] + qr * er[c, rows, zs]
                        value = value + wu[0, rows, :] * low[k : k + 1]
                        value = value + wu[2, rows, :] * high[k : k + 1]
                        if t == 0:
                            value = value + wu[1, rows, :] * low_edge[k : k + 1]
                        if t == 3:
                            value = value + wu[3, rows, :] * high_edge[k : k + 1]
                        if q == 0:
                            value = value + zpart[32 * k + 8 * t : 32 * k + 8 * t + 8, :128]
                        if q == 3:
                            value = value + zpart[32 * k + 8 * t : 32 * k + 8 * t + 8, 128:]
                        slots[slot, c, k, rows, zs] = value

        @pl.when(step == 0)
        def _():
            for c in range(5):
                slots[slot, c, 0] = slots[slot, c, 0] + (table[1, 0] * inner[0]) * fl[5 + c]

        @pl.when(step == B // GROUP - 1)
        def _():
            for c in range(5):
                slots[slot, c, GROUP - 1] = slots[slot, c, GROUP - 1] + (table[3, B - 1] * inner[1]) * fr[5 + c]

        copy_out(step).start()
        return carry

    lax.fori_loop(0, B // GROUP, group, 0)
    for slot in range(2):
        pltpu.make_async_copy(
            slots.at[slot], out.at[:, pl.ds(B - GROUP * (2 - slot), GROUP)], sems.at[slot]
        ).wait()


def finish(part, fl, fr, gl, gr, xr, xl, yr, yl, ghost):
    table = edge_weights()
    wy = np.broadcast_to(table[:, :, None], (4, B, 128))
    smem = pl.BlockSpec(memory_space=pltpu.SMEM)
    vmem = pl.BlockSpec(memory_space=pltpu.VMEM)
    return pl.pallas_call(
        finish_kernel,
        in_specs=[smem] + [vmem] * 12,
        out_specs=pl.BlockSpec(memory_space=pl.ANY),
        out_shape=jax.ShapeDtypeStruct((5, B, B, NZ), F32),
        scratch_shapes=[pltpu.VMEM((5, B, NZ), F32)] * 4
        + [pltpu.VMEM((4, B, 128), F32), pltpu.VMEM((2, 5, GROUP, B, NZ), F32), pltpu.SemaphoreType.DMA((2,))],
        compiler_params=pltpu.CompilerParams(vmem_limit_bytes=16 << 20),
        name="add_messages",
    )(
        jnp.asarray(table),
        part,
        fl,
        fr,
        gl,
        gr,
        xr,
        xl,
        yr,
        yl,
        jnp.asarray(wy),
        ghost,
        jnp.asarray(ghost_matrix()),
    )


def ring(array, axis, by):
    count = lax.axis_size(axis)
    return lax.ppermute(array, axis, [(i, (i + by) % count) for i in range(count)])


def rows_to_send(place_x, coarse, slot_rows, slot_times):
    devices = jnp.arange(16, dtype=jnp.int32)
    turn = (jnp.bitwise_xor(place_x, devices)[:, None] == devices[None, :]).astype(F32)
    both = jnp.concatenate([slot_rows, slot_times], axis=1).astype(F32)
    both = jnp.dot(turn, both, precision=highest)
    rows = both[:, :128] - (256 * place_x).astype(F32)
    weight = both[:, 128:] * 0.125
    mine = (rows >= 0.0) & (rows < 256.0)
    slots = jnp.arange(128)
    before = (slots[:, None] < slots[None, :]).astype(F32)
    rank = jnp.dot(mine.astype(F32), before, precision=highest)
    chosen = mine[:, None, :] & (rank[:, None, :] == jnp.arange(8, dtype=F32)[None, :, None])
    index = jnp.sum(jnp.where(chosen, rows[:, None, :], 0.0), axis=2)[:, :, None]
    late = jnp.sum(jnp.where(chosen, weight[:, None, :], 0.0), axis=2)[:, :, None]
    hit = index == jnp.arange(256, dtype=F32)[None, None, :]
    old = jnp.where(hit, 1.0 - late, 0.0)
    new = jnp.where(hit, late, 0.0)
    return jnp.einsum("dpr,rf->dpf", old, coarse[0], precision=highest) + jnp.einsum(
        "dpr,rf->dpf", new, coarse[1], precision=highest
    )


def trade(sent, bit):
    return lax.ppermute(sent, "gx", [(i, i ^ bit) for i in range(16)])


def slot_picks(place_x, slot_rows):
    own = lax.dynamic_index_in_dim(slot_rows, place_x, 0, keepdims=False)
    owner = own // 256
    slots = jnp.arange(128)
    same = (owner[:, None] == owner[None, :]) & (slots[None, :] < slots[:, None])
    rank = jnp.sum(same.astype(jnp.int32), axis=1)
    turn = jnp.bitwise_xor(owner, place_x)
    order = (turn // 4) * 4 + (turn % 2) * 2 + (turn // 2) % 2
    return (order[:, None] * 8 + rank[:, None] == slots[None, :]).astype(F32)


def local(density, momentum, energy, coarse_rows, ghost_rows, time_index):
    density, momentum, energy = (
        pltpu.with_memory_space_constraint(a, pltpu.HBM) for a in (density, momentum, energy)
    )
    place_x = lax.axis_index("gx")
    slot_rows = ghost_rows[0]
    rows = rows_to_send(place_x, coarse_rows[:, :, 0, :], slot_rows, time_index[0])
    pick = slot_picks(place_x, slot_rows)
    rows = rows.reshape(4, 2, 2, 8, 160)
    kept, sent = rows[:, 0].reshape(64, 160), rows[:, 1].reshape(64, 160)
    kept, sent, pick = lax.optimization_barrier((kept, sent, pick))
    got = trade(sent, 2)
    kept, sent = merge(kept, got, pick)
    got = trade(sent, 1)
    part, xr, xl, yr, yl = xy_part(density, momentum, energy, sent)
    kept, sent = merge(kept, got, xr)
    xr, xl, yr, yl, sent = lax.optimization_barrier((xr, xl, yr, yl, sent))
    fl = ring(xr, "gx", 1)
    fr = ring(xl, "gx", -1)
    gl = ring(yr, "gy", 1)
    gr = ring(yl, "gy", -1)
    got = trade(sent, 4)
    part = z_part(0, part, density, momentum, energy, sent)
    kept, sent = merge(kept, got, part)
    got = trade(sent, 8)
    part = z_part(2, part, density, momentum, energy, sent)
    ghost = ghost_flux(pick, kept, got)
    return finish(part, fl, fr, gl, gr, xr, xl, yr, yl, ghost)


def solution(mesh):
    return jax.shard_map(
        local,
        mesh=mesh,
        in_specs=(
            P("gx", "gy", None),
            P(None, "gx", "gy", None),
            P("gx", "gy", None),
            P(None, "gx", "gy", None),
            P("gy", None, None),
            P("gy", None, None),
        ),
        out_specs=P(None, "gx", "gy", None),
        check_vma=False,
    )
```

```python
import functools
import math

import jax
import jax.numpy as jnp
import ml_dtypes
import numpy as np
from jax import lax
from jax.experimental import pallas as pl
from jax.experimental.pallas import tpu as pltpu
from jax.sharding import PartitionSpec as P

BETA = 1.0 / 3.0
NEAR = 7.0 / 9.0
FAR = 1.0 / 36.0
STEP = 0.4
KAPPA = math.sqrt(1.0 - 4.0 * BETA * BETA)
ROOT = (-1.0 + KAPPA) / (2.0 * BETA)
TAIL = (NEAR * (1.0 / ROOT - ROOT) + FAR * (1.0 / ROOT**2 - ROOT**2)) / KAPPA
FIRST = (NEAR * (1.0 - ROOT**2) + FAR * (ROOT - ROOT**3)) / KAPPA
SCALE = 1.253065
B = 32
NZ = 512
F32 = jnp.float32
BF16 = jnp.bfloat16
highest = lax.Precision.HIGHEST


@functools.cache
def derivative_matrix(length):
    extended = np.zeros((length, length + 4))
    rows = np.arange(length)
    extended[rows, rows + 3] += NEAR
    extended[rows, rows + 1] -= NEAR
    extended[rows, rows + 4] += FAR
    extended[rows, rows] -= FAR
    left = np.eye(length) + BETA * (np.eye(length, k=1) + np.eye(length, k=-1))
    return np.linalg.solve(left, extended)


def rounded(matrix):
    return np.asarray(matrix, np.float32).astype(ml_dtypes.bfloat16)


def block_matrix(outer):
    place = np.arange(B)
    gap = place[None, :] - place[:, None]
    size = np.abs(gap).astype(float)
    entry = np.where(size == 0, 0.0, np.where(size == 1, FIRST, TAIL * ROOT**size))

    def spread(part):
        part = np.kron(np.eye(8), part) if outer else np.kron(part, np.eye(8))
        part = part.reshape(-1, 32, 1, 8)
        return np.concatenate([part, part], axis=2).reshape(-1, 512)

    right, left = ROOT ** (B - 1.0 - place), ROOT ** (place * 1.0)
    rows = [spread(np.sign(gap) * entry * SCALE)]
    rows += [spread(w[None]).astype(np.float32) for w in (right, left)]
    rows += [spread((w - rounded(w).astype(float))[None]) for w in (right, left)]
    rows += [spread((place == at)[None] * 1.0) for at in (B - 1, 0)]
    return rounded(np.concatenate(rows, axis=0))


def z_matrix():
    return rounded(derivative_matrix(NZ)[:, 2:-2].T * SCALE)


def ghost_matrix():
    full = derivative_matrix(NZ)
    table = np.zeros((4, 256))
    table[0:2, :128] = full[:128, 0:2].T
    table[2:4, 128:] = full[-128:, -2:].T
    table = np.asarray(-STEP * np.repeat(table, 8, axis=0), np.float32)
    high = rounded(table)
    low = rounded(table - high.astype(np.float32))
    return np.concatenate([high, high, low], axis=0)


def edge_weights():
    place = np.arange(B)
    table = np.zeros((4, B))
    table[0] = STEP * TAIL * ROOT ** (place + 1.0)
    table[1, 0] = STEP * (FIRST - TAIL * ROOT)
    table[2] = -STEP * TAIL * ROOT ** (B - place * 1.0)
    table[3, -1] = -STEP * (FIRST - TAIL * ROOT)
    return table.astype(np.float32)


def state_parts(density, m1, m2, m3, energy):
    inverse = 1.0 / density
    u1, u2, u3 = m1 * inverse, m2 * inverse, m3 * inverse
    pressure = 0.4 * energy - 0.2 * (m1 * u1 + m2 * u2 + m3 * u3)
    return u1, u2, u3, pressure


def split(value):
    high = value.astype(BF16)
    return high, (value - high.astype(F32)).astype(BF16)


def halves(value):
    high = value.astype(BF16).astype(F32)
    both = jnp.concatenate([high, value - high], axis=1).astype(BF16)
    return both.reshape(-1, 128)


PIECES = 7
ANYWHERE = pl.BlockSpec(memory_space=pl.ANY)
IN_VMEM = pl.BlockSpec(memory_space=pltpu.VMEM)


def in_hbm(array):
    return pltpu.with_memory_space_constraint(array, pltpu.HBM)


def piece_slices(k):
    xs = 2 * (k // 8)
    yh = (k // 4) % 2
    ys = pl.ds(pl.multiple_of(16 * yh, 16), 16)
    zs = pl.ds(pl.multiple_of(128 * (k % 4), 128), 128)
    return xs, yh, ys, zs


def load_pieces(state, xs, ys, zs):
    return tuple(state[c, xs, ys, zs].reshape(4, 8, 128) for c in range(5))


def keep(right, left, c, rows, result):
    extra = result[256:]
    right[c, rows] = extra[0:8] + extra[16:24]
    left[c, rows] = extra[8:16] + extra[24:32]
    right[5 + c, rows] = extra[32:40]
    left[5 + c, rows] = extra[40:48]


def y_kernel(first, *refs):
    rho, mom, ene, ky_in, after = refs[:5]
    state, part, fbuf, yr, yl, g0, g1, ky, sems = refs[-9:]
    factor = STEP / SCALE
    copies = []
    for i in range(2):
        xs = pl.ds(8 * (first + i), 8)
        copies.append(
            (
                pltpu.make_async_copy(rho.at[xs], state.at[0, xs], sems.at[i, 0]),
                pltpu.make_async_copy(mom.at[:, xs], state.at[1:4, xs], sems.at[i, 1]),
                pltpu.make_async_copy(ene.at[xs], state.at[4, xs], sems.at[i, 2]),
            )
        )
        for copy in copies[-1]:
            copy.start()

    matrix = pltpu.make_async_copy(ky_in, ky, sems.at[2, 0])
    matrix.start()

    def piece(i, k, gbuf):
        xp, yh, ys, zs = piece_slices(k)
        d, m1, m2, m3, e = load_pieces(state, pl.ds(8 * (first + i) + xp, 2), ys, zs)
        u1, u2, u3, p = state_parts(d, m1, m2, m3, e)
        ep = e + p
        cross = halves(m1 * u2)
        f = (halves(m1), halves(m1 * u1 + p), cross, halves(m3 * u1), halves(ep * u1))
        g = (halves(m2), cross, halves(m2 * u2 + p), halves(m3 * u2), halves(ep * u2))
        for c in range(5):
            for x2 in range(2):
                frow = pl.multiple_of(128 * (first + i) + 16 * xp + 16 * x2, 16)
                for y8 in range(2):
                    at = 32 * x2 + 16 * y8
                    fbuf[c, 2 * yh + y8, pl.ds(frow, 16), zs] = f[c][at : at + 16]
                row = pl.multiple_of(64 * xp + 64 * x2 + 32 * yh, 32)
                gbuf[c, pl.ds(row, 32), zs] = g[c][32 * x2 : 32 * x2 + 32]

    gs = (g0, g1)
    for i in range(3):
        if i < 2:
            for copy in copies[i]:
                copy.wait()
        if i == 1:
            matrix.wait()

        def stage(c, carry, i=i):
            if i < 2:
                for j in range(PIECES):
                    piece(i, jnp.minimum(PIECES * c + j, 31), gs[i % 2])
            if i >= 1:
                xs = pl.ds(8 * (first + i - 1), 8)
                across = jnp.dot(ky[...], gs[(i - 1) % 2][c], preferred_element_type=F32)
                part[c, xs] = state[c, xs] - factor * across[:256].reshape(8, B, NZ)
                keep(yr, yl, c, xs, across)
            return carry

        lax.fori_loop(0, 5, stage, 0)


def y_part(first, rho, mom, ene, after, begun=()):
    return pl.pallas_call(
        functools.partial(y_kernel, first),
        in_specs=[ANYWHERE] * 5 + [IN_VMEM] * len(begun),
        out_specs=[IN_VMEM] * 5,
        out_shape=[
            pltpu.VMEM((5, B, B, NZ), F32),
            pltpu.VMEM((5, B, B, NZ), F32),
            pltpu.VMEM((5, 4, 512, NZ), BF16),
            pltpu.VMEM((10, B, NZ), F32),
            pltpu.VMEM((10, B, NZ), F32),
        ],
        input_output_aliases={5 + i: i for i in range(len(begun))},
        scratch_shapes=[
            pltpu.VMEM((5, 512, NZ), BF16),
            pltpu.VMEM((5, 512, NZ), BF16),
            pltpu.VMEM((304, 512), BF16),
            pltpu.SemaphoreType.DMA((3, 3)),
        ],
        compiler_params=pltpu.CompilerParams(vmem_limit_bytes=12 << 20),
        name="y_part",
    )(rho, mom, ene, in_hbm(jnp.asarray(block_matrix(True))), after, *begun)


def x_kernel(start, fbuf, kx, after, part, xr, xl):
    factor = STEP / SCALE

    def component(c, carry):
        for block in range(4):
            ys = pl.ds(8 * block, 8)
            slope = jnp.dot(kx[...], fbuf[c, block], preferred_element_type=F32)
            part[c, :, ys, :] = part[c, :, ys, :] - factor * slope[:256].reshape(B, 8, NZ)
            keep(xr, xl, c, ys, slope)
        return carry

    lax.fori_loop(0, 5, component, 0)


def x_part(part, fbuf, after):
    return pl.pallas_call(
        x_kernel,
        in_specs=[IN_VMEM] * 3 + [ANYWHERE],
        out_specs=[IN_VMEM] * 3,
        out_shape=[pltpu.VMEM((5, B, B, NZ), F32)] + [pltpu.VMEM((10, B, NZ), F32)] * 2,
        input_output_aliases={0: 0},
        compiler_params=pltpu.CompilerParams(vmem_limit_bytes=6 << 20),
        name="x_part",
    )(part, fbuf, jnp.asarray(block_matrix(False)), after)


def z_kernel(start, state, mz, after, part, h0, h1):
    factor = STEP / SCALE

    def piece(i, k, hbuf):
        xp, yh, ys, zs = piece_slices(k)
        d, m1, m2, m3, e = load_pieces(state, pl.ds(8 * i + xp, 2), ys, zs)
        u1, u2, u3, p = state_parts(d, m1, m2, m3, e)
        h = [halves(v) for v in (m3, m1 * u3, m2 * u3, m3 * u3 + p, (e + p) * u3)]
        for c in range(5):
            for x2 in range(2):
                row = pl.multiple_of(64 * xp + 64 * x2 + 32 * yh, 32)
                hbuf[c, pl.ds(row, 32), zs] = h[c][32 * x2 : 32 * x2 + 32]

    hs = (h0, h1)
    for i in range(5):

        def stage(c, carry, i=i):
            along = []
            for j in range(PIECES):
                if i < 4:
                    piece(i, jnp.minimum(PIECES * c + j, 31), hs[i % 2])
                if i >= 1 and j in (1, 3):
                    rows = pl.ds(256 * len(along), 256)
                    both = jnp.dot(hs[(i - 1) % 2][c, rows], mz[...], preferred_element_type=F32)
                    both = both.reshape(16, 2, 8, NZ)
                    along.append(both[:, 0] + both[:, 1])
            for half, value in enumerate(along):
                xs = pl.ds(8 * (i - 1) + 4 * half, 4)
                part[c, xs] = part[c, xs] - factor * value.reshape(4, B, NZ)
            return carry

        lax.fori_loop(0, 5, stage, 0)


def z_part(part, state, after):
    return pl.pallas_call(
        z_kernel,
        in_specs=[IN_VMEM] * 3 + [ANYWHERE],
        out_specs=IN_VMEM,
        out_shape=pltpu.VMEM((5, B, B, NZ), F32),
        input_output_aliases={0: 0},
        scratch_shapes=[pltpu.VMEM((5, 512, NZ), BF16), pltpu.VMEM((5, 512, NZ), BF16)],
        compiler_params=pltpu.CompilerParams(vmem_limit_bytes=12 << 20),
        name="z_part",
    )(part, state, jnp.asarray(z_matrix()), after)


def merge_kernel(kept, got, after, stay, leave):
    for h, source in enumerate((kept, got)):
        for a in range(4):
            to = pl.ds(32 * h + 8 * a, 8)
            stay[to, :] = source[pl.ds(16 * a, 8), :]
            leave[to, :] = source[pl.ds(16 * a + 8, 8), :]


def merge(kept, got, after):
    return pl.pallas_call(
        merge_kernel,
        in_specs=[IN_VMEM] * 2 + [ANYWHERE],
        out_specs=[IN_VMEM] * 2,
        out_shape=[pltpu.VMEM((64, 160), F32)] * 2,
        compiler_params=pltpu.CompilerParams(vmem_limit_bytes=1 << 20),
        name="merge_rows",
    )(kept, got, after)


def ghost_kernel(pick, kept, got, out):
    ghosts = jnp.dot(pick[:, 0:64], kept[...], precision=highest, preferred_element_type=F32)
    ghosts = ghosts + jnp.dot(pick[:, 64:128], got[...], precision=highest, preferred_element_type=F32)
    d, m1, m2, m3, e = (ghosts[:, 32 * c : 32 * c + 32] for c in range(5))
    u1, u2, u3, p = state_parts(d, m1, m2, m3, e)
    cell = lax.broadcasted_iota(jnp.int32, (128, 256), 0) % 8
    lane = lax.broadcasted_iota(jnp.int32, (128, 256), 1) // 32
    for c, h in enumerate((m3, m1 * u3, m2 * u3, m3 * u3 + p, (e + p) * u3)):
        out[c] = jnp.where(cell == lane, jnp.concatenate([h] * 8, axis=1), 0.0)


def ghost_flux(pick, kept, got):
    return pl.pallas_call(
        ghost_kernel,
        in_specs=[IN_VMEM] * 3,
        out_specs=IN_VMEM,
        out_shape=pltpu.VMEM((5, 128, 256), F32),
        compiler_params=pltpu.CompilerParams(vmem_limit_bytes=4 << 20),
        name="ghost_flux",
    )(pick, kept, got)


GROUP = 8


def finish_kernel(table, part, fl, fr, gl, gr, xr, xl, yr, yl, wy, ghost, mg, out, el, er, hl, hr, wu, slots, sems):
    inner = []
    place = lax.axis_index("gx"), lax.axis_index("gy")
    for at_end, own, got, kept in (
        (place[0] == 0, xl, fl, el),
        (place[0] == 15, xr, fr, er),
        (place[1] == 0, yl, gl, hl),
        (place[1] == 7, yr, gr, hr),
    ):
        inner.append(jnp.where(at_end, 0.0, 1.0).astype(F32))

        @pl.when(at_end)
        def _(own=own, kept=kept):
            for c in range(5):
                kept[c] = ROOT * own[c] + ((FIRST - TAIL * ROOT) / TAIL) * own[5 + c]

        @pl.when(jnp.logical_not(at_end))
        def _(got=got, kept=kept):
            for c in range(5):
                kept[c] = got[c]

    wu[0] = wy[0]
    wu[1] = wy[1] * inner[2]
    wu[2] = wy[2]
    wu[3] = wy[3] * inner[3]

    def group(step, carry):
        slot = step % 2
        xs = pl.ds(GROUP * step, GROUP)

        def copy_out(at, c):
            return pltpu.make_async_copy(
                slots.at[slot, c], out.at[c, pl.ds(GROUP * at, GROUP)], sems.at[slot, c]
            )

        aligned = pl.ds(pl.multiple_of(GROUP * step, GROUP), GROUP)
        @pl.when(step >= 2)
        def _():
            for c in range(5):
                copy_out(step - 2, c).wait()

        for c in range(5):
            lines = [ghost[c, pl.ds(pl.multiple_of(32 * k + GROUP * step, 8), 8), :] for k in range(4)]
            high, low = split(jnp.concatenate(lines, axis=0))
            zpart = lax.dot_general(
                jnp.concatenate([high, low, high], axis=0),
                mg[...],
                (((0,), (0,)), ((), ())),
                preferred_element_type=F32,
            )
            for q in range(4):
                zs = pl.ds(128 * q, 128)
                low, high = hl[c, aligned, zs], hr[c, aligned, zs]
                low_edge, high_edge = gl[5 + c, aligned, zs], gr[5 + c, aligned, zs]
                for k in range(GROUP):
                    x = GROUP * step + k
                    ql = table[0, x]
                    qr = table[2, x]
                    for t in range(4):
                        rows = pl.ds(8 * t, 8)
                        value = part[c, x, rows, zs] + ql * el[c, rows, zs] + qr * er[c, rows, zs]
                        value = value + wu[0, rows, :] * low[k : k + 1]
                        value = value + wu[2, rows, :] * high[k : k + 1]
                        if k == 0:
                            value = value + (table[1, x] * inner[0]) * fl[5 + c, rows, zs]
                        if k == GROUP - 1:
                            value = value + (table[3, x] * inner[1]) * fr[5 + c, rows, zs]
                        if t == 0:
                            value = value + wu[1, rows, :] * low_edge[k : k + 1]
                        if t == 3:
                            value = value + wu[3, rows, :] * high_edge[k : k + 1]
                        if q == 0:
                            value = value + zpart[32 * k + 8 * t : 32 * k + 8 * t + 8, :128]
                        if q == 3:
                            value = value + zpart[32 * k + 8 * t : 32 * k + 8 * t + 8, 128:]
                        slots[slot, c, k, rows, zs] = value
            copy_out(step, c).start()
        return carry

    lax.fori_loop(0, B // GROUP, group, 0)
    for slot in range(2):
        for c in range(5):
            pltpu.make_async_copy(
                slots.at[slot, c], out.at[c, pl.ds(B - GROUP * (2 - slot), GROUP)], sems.at[slot, c]
            ).wait()


def finish(part, fl, fr, gl, gr, xr, xl, yr, yl, ghost):
    table = edge_weights()
    wy = np.broadcast_to(table[:, :, None], (4, B, 128))
    smem = pl.BlockSpec(memory_space=pltpu.SMEM)
    vmem = pl.BlockSpec(memory_space=pltpu.VMEM)
    return pl.pallas_call(
        finish_kernel,
        in_specs=[smem] + [vmem] * 12,
        out_specs=pl.BlockSpec(memory_space=pl.ANY),
        out_shape=jax.ShapeDtypeStruct((5, B, B, NZ), F32),
        scratch_shapes=[pltpu.VMEM((5, B, NZ), F32)] * 4
        + [pltpu.VMEM((4, B, 128), F32), pltpu.VMEM((2, 5, GROUP, B, NZ), F32), pltpu.SemaphoreType.DMA((2, 5))],
        compiler_params=pltpu.CompilerParams(vmem_limit_bytes=16 << 20),
        name="add_messages",
    )(
        jnp.asarray(table),
        part,
        fl,
        fr,
        gl,
        gr,
        xr,
        xl,
        yr,
        yl,
        jnp.asarray(wy),
        ghost,
        jnp.asarray(ghost_matrix()),
    )


def ring(array, axis, by):
    count = lax.axis_size(axis)
    return lax.ppermute(array, axis, [(i, (i + by) % count) for i in range(count)])


def choose_kernel(slots_in, times_in, coarse_in, kept, sent, pick, slots, times, coarse, sems):
    moves = [
        pltpu.make_async_copy(slots_in, slots, sems.at[0]),
        pltpu.make_async_copy(times_in, times, sems.at[1]),
        pltpu.make_async_copy(coarse_in, coarse, sems.at[2]),
    ]
    for move in moves:
        move.start()
    for move in moves:
        move.wait()
    place = lax.axis_index("gx")
    rows = slots[...].astype(F32)
    weight = times[...].astype(F32) * 0.125

    def iota(shape, axis):
        return lax.broadcasted_iota(jnp.int32, shape, axis)

    def exact(a, b, dims):
        return lax.dot_general(a, b, (dims, ((), ())), precision=highest, preferred_element_type=F32)

    item = iota((128, 16), 0) // 8
    turn = (item // 2 % 4) * 4 + (item // 8) * 2 + item % 2
    target = (jnp.bitwise_xor(turn, place) == iota((128, 16), 1)).astype(F32)
    begin = (256 * place).astype(F32)
    near = rows - begin
    mine = jnp.where((near >= 0.0) & (near < 256.0), 1.0, 0.0)
    before = (iota((128, 128), 0) < iota((128, 128), 1)).astype(F32)
    rank = exact(mine, before, ((1,), (0,)))
    spread = ((1,), (0,))
    chosen = exact(target, mine, spread) * jnp.where(
        exact(target, rank, spread) == (iota((128, 128), 0) % 8).astype(F32), 1.0, 0.0
    )
    index = jnp.sum(chosen * exact(target, near, spread), axis=1, keepdims=True)
    late = jnp.sum(chosen * exact(target, weight, spread), axis=1, keepdims=True)
    hit = index == iota((128, 256), 1).astype(F32)
    old = jnp.where(hit, 1.0 - late, 0.0)
    new = jnp.where(hit, late, 0.0)
    result = exact(old, coarse[0], ((1,), (1,))) + exact(new, coarse[1], ((1,), (1,)))
    kept[...] = result[:64]
    sent[...] = result[64:]

    self_row = (iota((8, 16), 1) == place).astype(F32)
    owner_row = exact(self_row, rows, spread)[0:1].astype(jnp.int32) // 256
    self_column = (iota((16, 128), 0) == place).astype(F32)
    owner = exact(rows, self_column, ((0,), (0,))).astype(jnp.int32) // 256
    same = (owner == owner_row) & (iota((128, 128), 1) < iota((128, 128), 0))
    order = jnp.sum(jnp.where(same, 1.0, 0.0), axis=1, keepdims=True)
    turn = jnp.bitwise_xor(owner, place)
    turn = (turn // 4) * 4 + (turn % 2) * 2 + (turn // 2) % 2
    pick[...] = jnp.where(turn * 8 + order.astype(jnp.int32) == iota((128, 128), 1), 1.0, 0.0)


def choose(slot_rows, slot_times, coarse):
    return pl.pallas_call(
        choose_kernel,
        in_specs=[ANYWHERE] * 3,
        out_specs=[IN_VMEM] * 3,
        out_shape=[pltpu.VMEM((64, 160), F32)] * 2 + [pltpu.VMEM((128, 128), F32)],
        scratch_shapes=[
            pltpu.VMEM((16, 128), jnp.int32),
            pltpu.VMEM((16, 128), jnp.int32),
            pltpu.VMEM((2, 160, 256), F32),
            pltpu.SemaphoreType.DMA((3,)),
        ],
        compiler_params=pltpu.CompilerParams(vmem_limit_bytes=6 << 20),
        name="choose_rows",
    )(*(in_hbm(a) for a in (slot_rows, slot_times, coarse)))


def trade(sent, bit):
    return lax.ppermute(sent, "gx", [(i, i ^ bit) for i in range(16)])


def local(density, momentum, energy, coarse_rows, ghost_rows, time_index):
    density, momentum, energy = (in_hbm(a) for a in (density, momentum, energy))
    cells = density, momentum, energy
    kept, sent, pick = choose(ghost_rows[0], time_index[0], coarse_rows[:, :, 0, :].transpose(0, 2, 1))
    got = trade(sent, 2)
    begun = y_part(0, *cells, sent)
    kept, sent = merge(kept, got, begun[3])
    got = trade(sent, 1)
    state, part, fbuf, yr, yl = y_part(2, *cells, sent, begun)
    kept, sent = merge(kept, got, yr)
    got = trade(sent, 4)
    part, xr, xl = x_part(part, fbuf, sent)
    kept, sent = merge(kept, got, xr)
    xr, xl, yr, yl, sent = lax.optimization_barrier((xr, xl, yr, yl, sent))
    fl = ring(xr, "gx", 1)
    fr = ring(xl, "gx", -1)
    gl = ring(yr, "gy", 1)
    gr = ring(yl, "gy", -1)
    got = trade(sent, 8)
    part = z_part(part, state, sent)
    ghost = ghost_flux(pick, kept, got)
    return finish(part, fl, fr, gl, gr, xr, xl, yr, yl, ghost)


def solution(mesh):
    return jax.shard_map(
        local,
        mesh=mesh,
        in_specs=(
            P("gx", "gy", None),
            P(None, "gx", "gy", None),
            P("gx", "gy", None),
            P(None, "gx", "gy", None),
            P("gy", None, None),
            P("gy", None, None),
        ),
        out_specs=P(None, "gx", "gy", None),
        check_vma=False,
    )
```

```python
import functools
import math

import jax
import jax.numpy as jnp
import ml_dtypes
import numpy as np
from jax import lax
from jax.experimental import pallas as pl
from jax.experimental.pallas import tpu as pltpu
from jax.sharding import PartitionSpec as P

BETA = 1.0 / 3.0
NEAR = 7.0 / 9.0
FAR = 1.0 / 36.0
STEP = 0.4
KAPPA = math.sqrt(1.0 - 4.0 * BETA * BETA)
ROOT = (-1.0 + KAPPA) / (2.0 * BETA)
TAIL = (NEAR * (1.0 / ROOT - ROOT) + FAR * (1.0 / ROOT**2 - ROOT**2)) / KAPPA
FIRST = (NEAR * (1.0 - ROOT**2) + FAR * (ROOT - ROOT**3)) / KAPPA
SCALE = 1.253065
B = 32
NZ = 512
F32 = jnp.float32
BF16 = jnp.bfloat16
highest = lax.Precision.HIGHEST


@functools.cache
def derivative_matrix(length):
    extended = np.zeros((length, length + 4))
    rows = np.arange(length)
    extended[rows, rows + 3] += NEAR
    extended[rows, rows + 1] -= NEAR
    extended[rows, rows + 4] += FAR
    extended[rows, rows] -= FAR
    left = np.eye(length) + BETA * (np.eye(length, k=1) + np.eye(length, k=-1))
    return np.linalg.solve(left, extended)


def rounded(matrix):
    return np.asarray(matrix, np.float32).astype(ml_dtypes.bfloat16)


def block_matrix(outer):
    place = np.arange(B)
    gap = place[None, :] - place[:, None]
    size = np.abs(gap).astype(float)
    entry = np.where(size == 0, 0.0, np.where(size == 1, FIRST, TAIL * ROOT**size))

    def spread(part):
        part = np.kron(np.eye(8), part) if outer else np.kron(part, np.eye(8))
        part = part.reshape(-1, 32, 1, 8)
        return np.concatenate([part, part], axis=2).reshape(-1, 512)

    right, left = ROOT ** (B - 1.0 - place), ROOT ** (place * 1.0)
    rows = [spread(np.sign(gap) * entry * SCALE)]
    rows += [spread(w[None]).astype(np.float32) for w in (right, left)]
    rows += [spread((w - rounded(w).astype(float))[None]) for w in (right, left)]
    rows += [spread((place == at)[None] * 1.0) for at in (B - 1, 0)]
    return rounded(np.concatenate(rows, axis=0))


def z_matrix():
    return rounded(derivative_matrix(NZ)[:, 2:-2].T * SCALE)


def ghost_matrix():
    full = derivative_matrix(NZ)
    table = np.zeros((4, 256))
    table[0:2, :128] = full[:128, 0:2].T
    table[2:4, 128:] = full[-128:, -2:].T
    table = np.asarray(-STEP * np.repeat(table, 8, axis=0), np.float32)
    high = rounded(table)
    low = rounded(table - high.astype(np.float32))
    return np.concatenate([high, high, low], axis=0)


def edge_weights():
    place = np.arange(B)
    table = np.zeros((4, B))
    table[0] = STEP * TAIL * ROOT ** (place + 1.0)
    table[1, 0] = STEP * (FIRST - TAIL * ROOT)
    table[2] = -STEP * TAIL * ROOT ** (B - place * 1.0)
    table[3, -1] = -STEP * (FIRST - TAIL * ROOT)
    return table.astype(np.float32)


def state_parts(density, m1, m2, m3, energy):
    inverse = 1.0 / density
    u1, u2, u3 = m1 * inverse, m2 * inverse, m3 * inverse
    pressure = 0.4 * energy - 0.2 * (m1 * u1 + m2 * u2 + m3 * u3)
    return u1, u2, u3, pressure


def split(value):
    high = value.astype(BF16)
    return high, (value - high.astype(F32)).astype(BF16)


def halves(value):
    high = value.astype(BF16).astype(F32)
    both = jnp.concatenate([high, value - high], axis=1).astype(BF16)
    return both.reshape(-1, 128)


PIECES = 7
ANYWHERE = pl.BlockSpec(memory_space=pl.ANY)
IN_VMEM = pl.BlockSpec(memory_space=pltpu.VMEM)


def in_hbm(array):
    return pltpu.with_memory_space_constraint(array, pltpu.HBM)


def piece_slices(k):
    xs = 2 * (k // 8)
    yh = (k // 4) % 2
    ys = pl.ds(pl.multiple_of(16 * yh, 16), 16)
    zs = pl.ds(pl.multiple_of(128 * (k % 4), 128), 128)
    return xs, yh, ys, zs


def load_pieces(state, xs, ys, zs):
    return tuple(state[c, xs, ys, zs].reshape(4, 8, 128) for c in range(5))


def keep(right, left, c, rows, result):
    extra = result[256:]
    right[c, rows] = extra[0:8] + extra[16:24]
    left[c, rows] = extra[8:16] + extra[24:32]
    right[5 + c, rows] = extra[32:40]
    left[5 + c, rows] = extra[40:48]


def y_kernel(first, *refs):
    rho, mom, ene, ky_in, after = refs[:5]
    state, part, fbuf, yr, yl, g0, g1, ky, sems = refs[-9:]
    factor = STEP / SCALE
    copies = []
    for i in range(2):
        xs = pl.ds(8 * (first + i), 8)
        copies.append(
            (
                pltpu.make_async_copy(rho.at[xs], state.at[0, xs], sems.at[i, 0]),
                pltpu.make_async_copy(mom.at[:, xs], state.at[1:4, xs], sems.at[i, 1]),
                pltpu.make_async_copy(ene.at[xs], state.at[4, xs], sems.at[i, 2]),
            )
        )
        for copy in copies[-1]:
            copy.start()

    matrix = pltpu.make_async_copy(ky_in, ky, sems.at[2, 0])
    matrix.start()

    def piece(i, k, gbuf):
        xp, yh, ys, zs = piece_slices(k)
        d, m1, m2, m3, e = load_pieces(state, pl.ds(8 * (first + i) + xp, 2), ys, zs)
        u1, u2, u3, p = state_parts(d, m1, m2, m3, e)
        ep = e + p
        cross = halves(m1 * u2)
        f = (halves(m1), halves(m1 * u1 + p), cross, halves(m3 * u1), halves(ep * u1))
        g = (halves(m2), cross, halves(m2 * u2 + p), halves(m3 * u2), halves(ep * u2))
        for c in range(5):
            for x2 in range(2):
                frow = pl.multiple_of(128 * (first + i) + 16 * xp + 16 * x2, 16)
                for y8 in range(2):
                    at = 32 * x2 + 16 * y8
                    fbuf[c, 2 * yh + y8, pl.ds(frow, 16), zs] = f[c][at : at + 16]
                row = pl.multiple_of(64 * xp + 64 * x2 + 32 * yh, 32)
                gbuf[c, pl.ds(row, 32), zs] = g[c][32 * x2 : 32 * x2 + 32]

    gs = (g0, g1)
    for i in range(3):
        if i < 2:
            for copy in copies[i]:
                copy.wait()
        if i == 1:
            matrix.wait()
        if i == 0:

            def opening(k, carry):
                for j in range(8):
                    piece(0, 8 * k + j, g0)
                return carry

            lax.fori_loop(0, 4, opening, 0)
            continue

        def stage(c, carry, i=i):
            if i < 2:
                for j in range(PIECES):
                    piece(i, jnp.minimum(PIECES * c + j, 31), gs[i % 2])
            if i >= 1:
                xs = pl.ds(8 * (first + i - 1), 8)
                across = jnp.dot(ky[...], gs[(i - 1) % 2][c], preferred_element_type=F32)
                part[c, xs] = state[c, xs] - factor * across[:256].reshape(8, B, NZ)
                keep(yr, yl, c, xs, across)
            return carry

        lax.fori_loop(0, 5, stage, 0)


def y_part(first, rho, mom, ene, after, begun=()):
    return pl.pallas_call(
        functools.partial(y_kernel, first),
        in_specs=[ANYWHERE] * 5 + [IN_VMEM] * len(begun),
        out_specs=[IN_VMEM] * 5,
        out_shape=[
            pltpu.VMEM((5, B, B, NZ), F32),
            pltpu.VMEM((5, B, B, NZ), F32),
            pltpu.VMEM((5, 4, 512, NZ), BF16),
            pltpu.VMEM((10, B, NZ), F32),
            pltpu.VMEM((10, B, NZ), F32),
        ],
        input_output_aliases={5 + i: i for i in range(len(begun))},
        scratch_shapes=[
            pltpu.VMEM((5, 512, NZ), BF16),
            pltpu.VMEM((5, 512, NZ), BF16),
            pltpu.VMEM((304, 512), BF16),
            pltpu.SemaphoreType.DMA((3, 3)),
        ],
        compiler_params=pltpu.CompilerParams(vmem_limit_bytes=12 << 20),
        name="y_part",
    )(rho, mom, ene, in_hbm(jnp.asarray(block_matrix(True))), after, *begun)


def x_kernel(start, fbuf, kx, after, part, xr, xl):
    factor = STEP / SCALE

    def component(c, carry):
        for block in range(4):
            ys = pl.ds(8 * block, 8)
            slope = jnp.dot(kx[...], fbuf[c, block], preferred_element_type=F32)
            part[c, :, ys, :] = part[c, :, ys, :] - factor * slope[:256].reshape(B, 8, NZ)
            keep(xr, xl, c, ys, slope)
        return carry

    lax.fori_loop(0, 5, component, 0)


def x_part(part, fbuf, after):
    return pl.pallas_call(
        x_kernel,
        in_specs=[IN_VMEM] * 3 + [ANYWHERE],
        out_specs=[IN_VMEM] * 3,
        out_shape=[pltpu.VMEM((5, B, B, NZ), F32)] + [pltpu.VMEM((10, B, NZ), F32)] * 2,
        input_output_aliases={0: 0},
        compiler_params=pltpu.CompilerParams(vmem_limit_bytes=6 << 20),
        name="x_part",
    )(part, fbuf, jnp.asarray(block_matrix(False)), after)


def z_kernel(start, state, mz, after, part, h0, h1):
    factor = STEP / SCALE

    def piece(i, k, hbuf):
        xp, yh, ys, zs = piece_slices(k)
        d, m1, m2, m3, e = load_pieces(state, pl.ds(8 * i + xp, 2), ys, zs)
        u1, u2, u3, p = state_parts(d, m1, m2, m3, e)
        h = [halves(v) for v in (m3, m1 * u3, m2 * u3, m3 * u3 + p, (e + p) * u3)]
        for c in range(5):
            for x2 in range(2):
                row = pl.multiple_of(64 * xp + 64 * x2 + 32 * yh, 32)
                hbuf[c, pl.ds(row, 32), zs] = h[c][32 * x2 : 32 * x2 + 32]

    def opening(k, carry):
        for j in range(8):
            piece(0, 8 * k + j, h0)
        return carry

    lax.fori_loop(0, 4, opening, 0)
    hs = (h0, h1)
    for i in range(1, 5):

        def stage(c, carry, i=i):
            along = []
            for j in range(PIECES):
                if i < 4:
                    piece(i, jnp.minimum(PIECES * c + j, 31), hs[i % 2])
                if i >= 1 and j in (1, 3):
                    rows = pl.ds(256 * len(along), 256)
                    both = jnp.dot(hs[(i - 1) % 2][c, rows], mz[...], preferred_element_type=F32)
                    both = both.reshape(16, 2, 8, NZ)
                    along.append(both[:, 0] + both[:, 1])
            for half, value in enumerate(along):
                xs = pl.ds(8 * (i - 1) + 4 * half, 4)
                part[c, xs] = part[c, xs] - factor * value.reshape(4, B, NZ)
            return carry

        lax.fori_loop(0, 5, stage, 0)


def z_part(part, state, after):
    return pl.pallas_call(
        z_kernel,
        in_specs=[IN_VMEM] * 3 + [ANYWHERE],
        out_specs=IN_VMEM,
        out_shape=pltpu.VMEM((5, B, B, NZ), F32),
        input_output_aliases={0: 0},
        scratch_shapes=[pltpu.VMEM((5, 512, NZ), BF16), pltpu.VMEM((5, 512, NZ), BF16)],
        compiler_params=pltpu.CompilerParams(vmem_limit_bytes=12 << 20),
        name="z_part",
    )(part, state, jnp.asarray(z_matrix()), after)


def merge_kernel(kept, got, after, stay, leave):
    for h, source in enumerate((kept, got)):
        for a in range(4):
            to = pl.ds(32 * h + 8 * a, 8)
            stay[to, :] = source[pl.ds(16 * a, 8), :]
            leave[to, :] = source[pl.ds(16 * a + 8, 8), :]


def merge(kept, got, after):
    return pl.pallas_call(
        merge_kernel,
        in_specs=[IN_VMEM] * 2 + [ANYWHERE],
        out_specs=[IN_VMEM] * 2,
        out_shape=[pltpu.VMEM((64, 160), F32)] * 2,
        compiler_params=pltpu.CompilerParams(vmem_limit_bytes=1 << 20),
        name="merge_rows",
    )(kept, got, after)


def ghost_kernel(pick, kept, got, out):
    ghosts = jnp.dot(pick[:, 0:64], kept[...], precision=highest, preferred_element_type=F32)
    ghosts = ghosts + jnp.dot(pick[:, 64:128], got[...], precision=highest, preferred_element_type=F32)
    d, m1, m2, m3, e = (ghosts[:, 32 * c : 32 * c + 32] for c in range(5))
    u1, u2, u3, p = state_parts(d, m1, m2, m3, e)
    cell = lax.broadcasted_iota(jnp.int32, (128, 256), 0) % 8
    lane = lax.broadcasted_iota(jnp.int32, (128, 256), 1) // 32
    for c, h in enumerate((m3, m1 * u3, m2 * u3, m3 * u3 + p, (e + p) * u3)):
        out[c] = jnp.where(cell == lane, jnp.concatenate([h] * 8, axis=1), 0.0)


def ghost_flux(pick, kept, got):
    return pl.pallas_call(
        ghost_kernel,
        in_specs=[IN_VMEM] * 3,
        out_specs=IN_VMEM,
        out_shape=pltpu.VMEM((5, 128, 256), F32),
        compiler_params=pltpu.CompilerParams(vmem_limit_bytes=4 << 20),
        name="ghost_flux",
    )(pick, kept, got)


GROUP = 8


def finish_kernel(table, part, fl, fr, gl, gr, xr, xl, yr, yl, wy, ghost, mg, out, el, er, hl, hr, wu, slots, sems):
    inner = []
    place = lax.axis_index("gx"), lax.axis_index("gy")
    for at_end, own, got, kept in (
        (place[0] == 0, xl, fl, el),
        (place[0] == 15, xr, fr, er),
        (place[1] == 0, yl, gl, hl),
        (place[1] == 7, yr, gr, hr),
    ):
        inner.append(jnp.where(at_end, 0.0, 1.0).astype(F32))

        @pl.when(at_end)
        def _(own=own, kept=kept):
            for c in range(5):
                kept[c] = ROOT * own[c] + ((FIRST - TAIL * ROOT) / TAIL) * own[5 + c]

        @pl.when(jnp.logical_not(at_end))
        def _(got=got, kept=kept):
            for c in range(5):
                kept[c] = got[c]

    wu[0] = wy[0]
    wu[1] = wy[1] * inner[2]
    wu[2] = wy[2]
    wu[3] = wy[3] * inner[3]

    def group(step, carry):
        slot = step % 2
        xs = pl.ds(GROUP * step, GROUP)

        def copy_out(at, c):
            return pltpu.make_async_copy(
                slots.at[slot, c], out.at[c, pl.ds(GROUP * at, GROUP)], sems.at[slot, c]
            )

        aligned = pl.ds(pl.multiple_of(GROUP * step, GROUP), GROUP)
        @pl.when(step >= 2)
        def _():
            for c in range(5):
                copy_out(step - 2, c).wait()

        for c in range(5):
            lines = [ghost[c, pl.ds(pl.multiple_of(32 * k + GROUP * step, 8), 8), :] for k in range(4)]
            high, low = split(jnp.concatenate(lines, axis=0))
            zpart = lax.dot_general(
                jnp.concatenate([high, low, high], axis=0),
                mg[...],
                (((0,), (0,)), ((), ())),
                preferred_element_type=F32,
            )
            for q in range(4):
                zs = pl.ds(128 * q, 128)
                low, high = hl[c, aligned, zs], hr[c, aligned, zs]
                low_edge, high_edge = gl[5 + c, aligned, zs], gr[5 + c, aligned, zs]
                for k in range(GROUP):
                    x = GROUP * step + k
                    ql = table[0, x]
                    qr = table[2, x]
                    for t in range(4):
                        rows = pl.ds(8 * t, 8)
                        value = part[c, x, rows, zs] + ql * el[c, rows, zs] + qr * er[c, rows, zs]
                        value = value + wu[0, rows, :] * low[k : k + 1]
                        value = value + wu[2, rows, :] * high[k : k + 1]
                        if k == 0:
                            value = value + (table[1, x] * inner[0]) * fl[5 + c, rows, zs]
                        if k == GROUP - 1:
                            value = value + (table[3, x] * inner[1]) * fr[5 + c, rows, zs]
                        if t == 0:
                            value = value + wu[1, rows, :] * low_edge[k : k + 1]
                        if t == 3:
                            value = value + wu[3, rows, :] * high_edge[k : k + 1]
                        if q == 0:
                            value = value + zpart[32 * k + 8 * t : 32 * k + 8 * t + 8, :128]
                        if q == 3:
                            value = value + zpart[32 * k + 8 * t : 32 * k + 8 * t + 8, 128:]
                        slots[slot, c, k, rows, zs] = value
            copy_out(step, c).start()
        return carry

    lax.fori_loop(0, B // GROUP, group, 0)
    for slot in range(2):
        for c in range(5):
            pltpu.make_async_copy(
                slots.at[slot, c], out.at[c, pl.ds(B - GROUP * (2 - slot), GROUP)], sems.at[slot, c]
            ).wait()


def finish(part, fl, fr, gl, gr, xr, xl, yr, yl, ghost):
    table = edge_weights()
    wy = np.broadcast_to(table[:, :, None], (4, B, 128))
    smem = pl.BlockSpec(memory_space=pltpu.SMEM)
    vmem = pl.BlockSpec(memory_space=pltpu.VMEM)
    return pl.pallas_call(
        finish_kernel,
        in_specs=[smem] + [vmem] * 12,
        out_specs=pl.BlockSpec(memory_space=pl.ANY),
        out_shape=jax.ShapeDtypeStruct((5, B, B, NZ), F32),
        scratch_shapes=[pltpu.VMEM((5, B, NZ), F32)] * 4
        + [pltpu.VMEM((4, B, 128), F32), pltpu.VMEM((2, 5, GROUP, B, NZ), F32), pltpu.SemaphoreType.DMA((2, 5))],
        compiler_params=pltpu.CompilerParams(vmem_limit_bytes=16 << 20),
        name="add_messages",
    )(
        jnp.asarray(table),
        part,
        fl,
        fr,
        gl,
        gr,
        xr,
        xl,
        yr,
        yl,
        jnp.asarray(wy),
        ghost,
        jnp.asarray(ghost_matrix()),
    )


def ring(array, axis, by):
    count = lax.axis_size(axis)
    return lax.ppermute(array, axis, [(i, (i + by) % count) for i in range(count)])


def choose_kernel(slots_in, times_in, coarse_in, kept, sent, pick, slots, times, coarse, sems):
    moves = [
        pltpu.make_async_copy(slots_in, slots, sems.at[0]),
        pltpu.make_async_copy(times_in, times, sems.at[1]),
        pltpu.make_async_copy(coarse_in, coarse, sems.at[2]),
    ]
    for move in moves:
        move.start()
    for move in moves:
        move.wait()
    place = lax.axis_index("gx")
    rows = slots[...].astype(F32)
    weight = times[...].astype(F32) * 0.125

    def iota(shape, axis):
        return lax.broadcasted_iota(jnp.int32, shape, axis)

    def exact(a, b, dims):
        return lax.dot_general(a, b, (dims, ((), ())), precision=highest, preferred_element_type=F32)

    item = iota((128, 16), 0) // 8
    turn = (item // 2 % 4) * 4 + (item // 8) * 2 + item % 2
    target = (jnp.bitwise_xor(turn, place) == iota((128, 16), 1)).astype(F32)
    begin = (256 * place).astype(F32)
    near = rows - begin
    mine = jnp.where((near >= 0.0) & (near < 256.0), 1.0, 0.0)
    before = (iota((128, 128), 0) < iota((128, 128), 1)).astype(F32)
    rank = exact(mine, before, ((1,), (0,)))
    spread = ((1,), (0,))
    chosen = exact(target, mine, spread) * jnp.where(
        exact(target, rank, spread) == (iota((128, 128), 0) % 8).astype(F32), 1.0, 0.0
    )
    index = jnp.sum(chosen * exact(target, near, spread), axis=1, keepdims=True)
    late = jnp.sum(chosen * exact(target, weight, spread), axis=1, keepdims=True)
    hit = index == iota((128, 256), 1).astype(F32)
    old = jnp.where(hit, 1.0 - late, 0.0)
    new = jnp.where(hit, late, 0.0)
    result = exact(old, coarse[0], ((1,), (1,))) + exact(new, coarse[1], ((1,), (1,)))
    kept[...] = result[:64]
    sent[...] = result[64:]

    self_row = (iota((8, 16), 1) == place).astype(F32)
    owner_row = exact(self_row, rows, spread)[0:1].astype(jnp.int32) // 256
    self_column = (iota((16, 128), 0) == place).astype(F32)
    owner = exact(rows, self_column, ((0,), (0,))).astype(jnp.int32) // 256
    same = (owner == owner_row) & (iota((128, 128), 1) < iota((128, 128), 0))
    order = jnp.sum(jnp.where(same, 1.0, 0.0), axis=1, keepdims=True)
    turn = jnp.bitwise_xor(owner, place)
    turn = (turn // 4) * 4 + (turn % 2) * 2 + (turn // 2) % 2
    pick[...] = jnp.where(turn * 8 + order.astype(jnp.int32) == iota((128, 128), 1), 1.0, 0.0)


def choose(slot_rows, slot_times, coarse):
    return pl.pallas_call(
        choose_kernel,
        in_specs=[ANYWHERE] * 3,
        out_specs=[IN_VMEM] * 3,
        out_shape=[pltpu.VMEM((64, 160), F32)] * 2 + [pltpu.VMEM((128, 128), F32)],
        scratch_shapes=[
            pltpu.VMEM((16, 128), jnp.int32),
            pltpu.VMEM((16, 128), jnp.int32),
            pltpu.VMEM((2, 160, 256), F32),
            pltpu.SemaphoreType.DMA((3,)),
        ],
        compiler_params=pltpu.CompilerParams(vmem_limit_bytes=6 << 20),
        name="choose_rows",
    )(*(in_hbm(a) for a in (slot_rows, slot_times, coarse)))


def trade(sent, bit):
    return lax.ppermute(sent, "gx", [(i, i ^ bit) for i in range(16)])


def local(density, momentum, energy, coarse_rows, ghost_rows, time_index):
    density, momentum, energy = (in_hbm(a) for a in (density, momentum, energy))
    cells = density, momentum, energy
    kept, sent, pick = choose(ghost_rows[0], time_index[0], coarse_rows[:, :, 0, :].transpose(0, 2, 1))
    got = trade(sent, 2)
    begun = y_part(0, *cells, sent)
    kept, sent = merge(kept, got, begun[3])
    got = trade(sent, 1)
    state, part, fbuf, yr, yl = y_part(2, *cells, sent, begun)
    kept, sent = merge(kept, got, yr)
    got = trade(sent, 4)
    part, xr, xl = x_part(part, fbuf, sent)
    kept, sent = merge(kept, got, xr)
    xr, xl, yr, yl, sent = lax.optimization_barrier((xr, xl, yr, yl, sent))
    fl = ring(xr, "gx", 1)
    fr = ring(xl, "gx", -1)
    gl = ring(yr, "gy", 1)
    gr = ring(yl, "gy", -1)
    got = trade(sent, 8)
    part = z_part(part, state, sent)
    ghost = ghost_flux(pick, kept, got)
    return finish(part, fl, fr, gl, gr, xr, xl, yr, yl, ghost)


def solution(mesh):
    return jax.shard_map(
        local,
        mesh=mesh,
        in_specs=(
            P("gx", "gy", None),
            P(None, "gx", "gy", None),
            P("gx", "gy", None),
            P(None, "gx", "gy", None),
            P("gy", None, None),
            P("gy", None, None),
        ),
        out_specs=P(None, "gx", "gy", None),
        check_vma=False,
    )
```
